128 devices in a mesh: row: 8 (over y, core), col: 16 (over x, z).
Axes of the slice: x: 4, y: 4, z: 4, core: 2. Of those that a mesh axis runs over, the one named last changes fastest.
Arguments:
- trail_rows: bfloat16 [24576, 8192], P('row', 'col'), may hold values from -0.0390625 to 0.0390625
- rows_first: bfloat16 [512, 8192], P(None, 'col'), may hold values from -0.25 to 0.25
- rows_second: bfloat16 [512, 8192], P(None, 'col'), may hold values from -0.25 to 0.25
- diag_first: float32 [512, 512], replicated, may hold values from -0.25 to 4, as said below
- diag_second: float32 [512, 512], replicated, may hold values from -0.25 to 4, as said below
- sub_block: float32 [512, 512], replicated, may hold values from -0.25 to 0.25
- cot_first: float32 [24576, 512], P('row', 'col'), may hold values from -6 to 6
- cot_second: float32 [24576, 512], P('row', 'col'), may hold values from -6 to 6
- cot_trail: float32 [24576, 8192], P('row', 'col'), may hold values from -6 to 6
- cot_rows_first: float32 [512, 8192], P('row', 'col'), may hold values from -6 to 6
- cot_rows_second: float32 [512, 8192], P('row', 'col'), may hold values from -6 to 6
Outputs:
- new_trail: float32 [24576, 8192], P('row', 'col')
- new_rows_first: float32 [512, 8192], P('row', 'col')
- new_rows_second: float32 [512, 8192], P('row', 'col')
- solved_first: float32 [24576, 512], P('row', 'col')
- solved_second: float32 [24576, 512], P('row', 'col')
The draws below stay inside these ranges and needn't reach their ends.
Inputs may be any that keep to these rules, and one draw needn't show every extreme that they name: `diag_first`: lower triangular; the diagonal lies between 1 and 4, entries above it are zero. `diag_second`: lower triangular; the diagonal lies between 1 and 4, entries above it are zero.
All inputs are finite; a program needn't handle non-finite values.
Results may differ from the reference program's by a relative error of at most 0.0021.
Values sent between devices are 32-bit elements; how exact they have to be, the bound alone decides.
A program may use at most 128 MiB of HBM per device.

```python
import jax
import jax.numpy as jnp
from jax import lax

NB = 512
MROWS = 24576
KCOLS = 8192


def factor_draw(key):
    key_diag, key_off = jax.random.split(key)
    values = jnp.exp(jax.random.uniform(key_diag, (NB,), jnp.float32, 0.0, jnp.log(3.0)))
    off_part = jnp.clip(jax.random.normal(key_off, (NB, NB), jnp.float32) * (0.6 / NB ** 0.5), -0.25, 0.25)
    return jnp.tril(off_part, -1) + jnp.diag(values)


def draw_diag_first(key, part):
    return factor_draw(jax.random.fold_in(key, 11))


def draw_diag_second(key, part):
    return factor_draw(jax.random.fold_in(key, 23))


def block_scale(stream_key, extent, cuts, least, top_value):
    factor_of, own = 1.0, jax.random.fold_in(stream_key, 6)
    for dim, shards_of in cuts:
        draws = jnp.exp(jax.random.uniform(jax.random.fold_in(own, dim), (shards_of,), jnp.float32, least / len(cuts), top_value / len(cuts)))
        factor_of = factor_of * jnp.repeat(draws, extent[dim] // shards_of).reshape([-1 if axis == dim else 1 for axis in range(len(extent))])
    return factor_of


def gaussian(stream_key, dims, scale, most, shards=(), dtype=jnp.bfloat16):
    array = scale * jax.random.normal(stream_key, dims, jnp.float32)
    if shards:
        array = array * block_scale(stream_key, dims, shards, -0.22, 0.18)
    return jnp.clip(array, -most, most).astype(dtype)


def setup_inputs(seed: int = 0) -> dict:
    keys = jax.random.split(jax.random.key(seed), 12)
    return {
        "trail_rows": gaussian(keys[0], (MROWS, KCOLS), MROWS ** -0.5, 0.0390625, ((0, 8), (1, 16))),
        "rows_first": gaussian(keys[1], (NB, KCOLS), NB ** -0.5, 0.25, ((1, 16),)),
        "rows_second": gaussian(keys[2], (NB, KCOLS), NB ** -0.5, 0.25, ((1, 16),)),
        "diag_first": draw_diag_first(jax.random.fold_in(keys[11], 71), 0),
        "diag_second": draw_diag_second(jax.random.fold_in(keys[11], 71), 0),
        "sub_block": gaussian(keys[5], (NB, NB), NB ** -0.5, 0.25, (), jnp.float32),
        "cot_first": gaussian(keys[6], (MROWS, NB), 1.0, 6.0, ((0, 8), (1, 16)), jnp.float32),
        "cot_second": gaussian(keys[7], (MROWS, NB), 1.0, 6.0, ((0, 8), (1, 16)), jnp.float32),
        "cot_trail": gaussian(keys[8], (MROWS, KCOLS), 1.0, 6.0, ((0, 8), (1, 16)), jnp.float32),
        "cot_rows_first": gaussian(keys[9], (NB, KCOLS), 1.0, 6.0, ((0, 8), (1, 16)), jnp.float32),
        "cot_rows_second": gaussian(keys[10], (NB, KCOLS), 1.0, 6.0, ((0, 8), (1, 16)), jnp.float32),
    }


def solve_right(cotangent, factor):
    return lax.linalg.triangular_solve(factor, cotangent, left_side=False, lower=True)

def reference(trail_rows, rows_first, rows_second, diag_first, diag_second, sub_block, cot_first, cot_second, cot_trail, cot_rows_first, cot_rows_second):
    solved_second = solve_right(cot_second, diag_second)
    carried = cot_first - jnp.dot(solved_second.astype(jnp.float32), sub_block.astype(jnp.float32), precision=lax.Precision.HIGHEST, preferred_element_type=jnp.float32)
    solved_first = solve_right(carried, diag_first)
    low_first = solved_first.astype(jnp.bfloat16)
    low_second = solved_second.astype(jnp.bfloat16)
    update = jnp.dot(low_second.astype(jnp.float32), rows_second.astype(jnp.float32), preferred_element_type=jnp.float32) + jnp.dot(low_first.astype(jnp.float32), rows_first.astype(jnp.float32), preferred_element_type=jnp.float32)
    new_trail = cot_trail - update
    new_rows_first = cot_rows_first - jnp.dot(low_first.T.astype(jnp.float32), trail_rows.astype(jnp.float32), preferred_element_type=jnp.float32)
    new_rows_second = cot_rows_second - jnp.dot(low_second.T.astype(jnp.float32), trail_rows.astype(jnp.float32), preferred_element_type=jnp.float32)
    return (new_trail, new_rows_first, new_rows_second, solved_first, solved_second)
```

```python
import functools

import jax
import jax.numpy as jnp
from jax import lax
from jax.experimental import pallas as pl
from jax.experimental.pallas import tpu as pltpu
from jax.sharding import PartitionSpec as P

MESH = pl.DeviceIdType.MESH
BF = jnp.bfloat16
F32 = jnp.float32
W = 512
OFF = 2
NB = 512
HALF = NB // 2


def split(value):
    high = value.astype(BF)
    return high, (value - high.astype(F32)).astype(BF)


def dot(left, right):
    return jnp.dot(left, right, preferred_element_type=F32)


def dot3(left, right):
    lh, ll = left
    rh, rl = right
    return dot(lh, rh) + (dot(lh, rl) + dot(ll, rh))


def dot_tall(stacked, right):
    rh, rl = right
    rows = stacked.shape[0] // 2
    both = dot(stacked, rh)
    return both[:rows] + (both[rows:] + dot(stacked[:rows], rl))


def invert_lower(block):
    base, groups = 32, 4
    row = lax.broadcasted_iota(jnp.int32, (base, 128), 0)
    lane = lax.broadcasted_iota(jnp.int32, (base, 128), 1)
    group = lane // base
    first = group * base
    halves = []
    packs = []
    for half in range(2):
        part = block[128 * half : 128 * half + 128, 128 * half : 128 * half + 128]
        pack = jnp.zeros((base, 128), F32)
        for q in range(groups):
            pack = jnp.where(group == q, part[base * q : base * q + base], pack)
        packs.append(pack)
    pack = jnp.concatenate(packs, axis=0)
    row2, lane2, first2 = (jnp.concatenate([v, v], axis=0) for v in (row, lane, first))
    on_diag = row2 == lane2 - first2
    diag_cols = jnp.where(on_diag, pack, 0.0)
    diag_rows = jnp.take_along_axis(pack, first2 + row2, axis=1)
    unit = jnp.where(lane2 - first2 < row2, pack / diag_rows, 0.0)
    inv = jnp.where(on_diag, 1.0, 0.0).astype(F32)
    for k in range(base - 1):
        column = jnp.take_along_axis(unit, first2 + k, axis=1)
        pivot = jnp.concatenate(
            [jnp.broadcast_to(inv[k + base * h : k + base * h + 1], (base, 128)) for h in range(2)], axis=0
        )
        inv = inv - column * pivot
    pieces = []
    for half in range(2):
        mine = slice(base * half, base * half + base)
        scale = jnp.sum(diag_cols[mine], axis=0, keepdims=True)
        scaled = inv[mine] / scale
        full = jnp.concatenate([jnp.where(group == q, scaled, 0.0) for q in range(groups)], axis=0)
        zero = jnp.zeros((128, 128), F32)
        pieces.append(jnp.concatenate([full, zero] if half == 0 else [zero, full], axis=1))
    result = jnp.concatenate(pieces, axis=0)
    brow = lax.broadcasted_iota(jnp.int32, (HALF, HALF), 0)
    bcol = lax.broadcasted_iota(jnp.int32, (HALF, HALF), 1)
    for size in (32, 64, 128):
        below = (brow // size == bcol // size + 1) & (lax.rem(bcol // size, 2) == 0)
        low = jnp.where(below, block, 0.0)
        parts = split(result)
        result = result - dot3(parts, split(dot3(split(low), parts)))
    return result


def kernel(
    cs_ref, cf_ref, trail_ref, rs_ref, rf_ref, ds_ref, df_ref, e_ref, ct_ref, crf_ref, crs_ref,
    nt_ref, nrf_ref, nrs_ref, sf_ref, ss_ref,
    G, T, L, CT, TR, R, D, E, acc, XB, PB, HB, FB, CR, XS, inv_s, off_s, e_s,
    lsem, isem, osem, ssem, rsem, rs_send, rs_recv,
):
    K = G.shape[0] // 2
    N = 2 * K
    c = lax.axis_index("col")
    r = lax.axis_index("row")
    x, z = c // 4, lax.rem(c, 4)
    y, core = r // 2, lax.rem(r, 2)
    x_p, x_m = lax.rem(x + 1, 4), lax.rem(x + 3, 4)
    z_p, z_m = lax.rem(z + 1, 4), lax.rem(z + 3, 4)
    y_p, y_m = lax.rem(y + 1, 4), lax.rem(y + 3, 4)
    to = (
        ({"col": x_p * 4 + z, "row": r}, {"col": x_m * 4 + z, "row": r}),
        ({"col": x * 4 + z_p, "row": r}, {"col": x * 4 + z_m, "row": r}),
        ({"col": c, "row": 2 * y_p + core}, {"col": c, "row": 2 * y_m + core}),
    )
    other = {"col": c, "row": 2 * y + 1 - core}

    def own(g, source):
        k = lax.rem(g, K)
        lanes = pl.ds(pl.multiple_of(k * W, 128), W)
        return pltpu.make_async_copy(source.at[:, lanes], G.at[g, x, z], lsem.at[g])

    @pl.loop(0, K)
    def _(k):
        own(k, cs_ref).start()

    @pl.loop(0, K)
    def _(k):
        own(k + K, cf_ref).start()

    loads = [
        pltpu.make_async_copy(ds_ref, D.at[0], isem.at[0]),
        pltpu.make_async_copy(df_ref, D.at[1], isem.at[1]),
        pltpu.make_async_copy(e_ref, E, isem.at[2]),
        pltpu.make_async_copy(trail_ref, TR, isem.at[3]),
        pltpu.make_async_copy(rs_ref, R.at[:NB], isem.at[4]),
        pltpu.make_async_copy(rf_ref, R.at[NB:], isem.at[5]),
        pltpu.make_async_copy(crs_ref, CR.at[0], isem.at[6]),
        pltpu.make_async_copy(crf_ref, CR.at[1], isem.at[7]),
        pltpu.make_async_copy(ct_ref, CT, isem.at[8]),
    ]
    for load in loads:
        load.start()

    barrier = pltpu.get_barrier_semaphore()
    for pair in to:
        for device in pair:
            pl.semaphore_signal(barrier, 1, device_id=device, device_id_type=MESH)
    pl.semaphore_signal(barrier, 1, device_id=other, device_id_type=MESH)
    pl.semaphore_wait(barrier, 7)

    def hop(g, t, s, d, landing):
        i1, m1, p1 = ((x, x_m, x_p), (z, z_m, z_p))[t]
        i2, m2, p2 = ((z, z_m, z_p), (x, x_m, x_p))[t]
        near = lambda mine, minus, plus: (minus if d == 0 else plus)
        opposite = lambda mine: lax.rem(mine + 2, 4)
        rows, half = pl.ds(16 * t, 16), pl.ds(16 * t + 8 * d, 8)
        every = slice(None)
        if s == 0:
            a, b, part = (near(i1, m1, p1) if landing else i1), i2, rows
        elif s == 1:
            a, b, part = (opposite(i1) if landing else near(i1, m1, p1)), i2, half
        elif s == 2:
            a, b, part = every, (near(i2, m2, p2) if landing else i2), rows
        else:
            a, b, part = every, (opposite(i2) if landing else near(i2, m2, p2)), half
        ref = G.at[g, a, b, part] if t == 0 else G.at[g, b, a, part]
        axis = t if s < 2 else 1 - t
        index = t * 8 + s * 2 + d
        return pltpu.make_async_remote_copy(
            ref, ref, ssem.at[g, index], rsem.at[g, index], device_id=to[axis][d], device_id_type=MESH
        )

    def stage(g, s):
        if s == 0:
            own(g, cs_ref).wait()
        else:
            for t in range(2):
                for d in range(2):
                    hop(g, t, s - 1, d, True).wait_recv()
        if s < 4:
            for t in range(2):
                for d in range(2):
                    hop(g, t, s, d, False).start()

    def communicate(tick):
        for s in (3, 2, 1, 0, 4):
            g = tick - s * OFF
            if isinstance(tick, int):
                if 0 <= g < N:
                    stage(g, s)
            else:

                @pl.when((g >= 0) & (g < N))
                def _():
                    stage(g, s)

    communicate(0)
    loads[0].wait()
    loads[1].wait()
    communicate(1)

    @pl.loop(0, 4)
    def _(j):
        communicate(2 + j)
        panel, at = j // 2, pl.multiple_of(lax.rem(j, 2) * HALF, HALF)
        inverse = invert_lower(D[panel, pl.ds(at, HALF), pl.ds(at, HALF)])
        high, low = split(inverse.T)
        inv_s[j, :HALF] = high
        inv_s[j, HALF:] = low

    loads[2].wait()
    for panel in range(2):
        high, low = split(D[panel, HALF:, :HALF].T)
        off_s[panel, :HALF] = high
        off_s[panel, HALF:] = low
    high, low = split(E[...].T)
    e_s[:NB] = high
    e_s[NB:] = low
    acc[...] = jnp.zeros_like(acc)
    for load in loads[3:]:
        load.wait()
    for tick in range(6, 4 * OFF):
        communicate(tick)

    def solve(right, panel):
        x1 = dot_tall(inv_s[2 * panel + 1], split(right[HALF:]))
        x1_parts = split(x1)
        left = right[:HALF] - dot_tall(off_s[panel], x1_parts)
        x0 = dot_tall(inv_s[2 * panel], split(left))
        return x0, x1, split(x0), x1_parts

    def put(k, panel, solved, out_ref):
        x0, x1, (h0, _), (h1, _) = solved
        XS[:HALF] = x0
        XS[HALF:] = x1
        lanes = pl.ds(pl.multiple_of(k * W, 128), W)
        out_ref[:, lanes] = XS[pl.ds(pl.multiple_of(c * 32, 32), 32)]
        L[k, NB * panel : NB * panel + HALF] = h0
        L[k, NB * panel + HALF : NB * panel + NB] = h1
        rows = TR[pl.ds(pl.multiple_of(k * W, 128), W)]
        for q in range(2):
            part = slice(HALF * q, HALF * q + HALF)
            acc[panel, part] += dot((h0, h1)[q], rows)

    def reduce_copies(panel, s):
        base = panel * 5
        make = pltpu.make_async_remote_copy

        def remote(src, dst, i, device):
            return make(src, dst, rs_send.at[base + i], rs_recv.at[base + i], device_id=device, device_id_type=MESH)

        if s == 0:
            return [remote(PB.at[panel, 1], XB.at[panel], 0, other)]
        far = lax.rem(y + 2, 4)
        if s == 1:
            return [
                remote(PB.at[panel, 0, far, :32], HB.at[panel, 0], 1, to[2][0]),
                remote(PB.at[panel, 0, far, 32:], HB.at[panel, 1], 2, to[2][1]),
            ]
        return [
            remote(PB.at[panel, 0, y_p], FB.at[panel, 0], 3, to[2][0]),
            remote(PB.at[panel, 0, y_m], FB.at[panel, 1], 4, to[2][1]),
        ]

    def reduce_step(panel, s, out_ref):
        if s == 0:
            for q in range(4):
                PB[panel, 0, q] = acc[panel, pl.ds(pl.multiple_of(128 * q + 64 * core, 64), 64)]
                PB[panel, 1, q] = acc[panel, pl.ds(pl.multiple_of(128 * q + 64 * (1 - core), 64), 64)]
        elif s == 1:
            for copy in reduce_copies(panel, 0):
                copy.wait_recv()
            PB[panel, 0] += XB[panel]
        elif s == 2:
            for copy in reduce_copies(panel, 1):
                copy.wait_recv()
            PB[panel, 0, y_p, :32] += HB[panel, 0]
            PB[panel, 0, y_m, 32:] += HB[panel, 1]
        else:
            for copy in reduce_copies(panel, 2):
                copy.wait_recv()
            out_ref[...] = CR[panel] - ((PB[panel, 0, y] + FB[panel, 0]) + FB[panel, 1])
        if s < 3:
            for copy in reduce_copies(panel, s):
                copy.start()

    def store(k):
        rows = pl.ds(pl.multiple_of(k * W, W), W)
        return pltpu.make_async_copy(CT.at[rows], nt_ref.at[rows], osem.at[k])

    def trail(k):
        rows = pl.ds(pl.multiple_of(k * W, W), W)
        update = lax.dot_general(L[k], R[...], (((0,), (0,)), ((), ())), preferred_element_type=F32)
        CT[rows] -= update
        store(k).start()

    @pl.loop(0, K)
    def _(k):
        communicate(4 * OFF + k)
        solved = solve(G[k].reshape(NB, W), 0)
        put(k, 0, solved, ss_ref)
        T[k] = dot_tall(e_s[...], tuple(jnp.concatenate(p, axis=0) for p in zip(solved[2], solved[3])))

    @pl.loop(0, K)
    def _(k):
        communicate(4 * OFF + K + k)
        for s in range(4):

            @pl.when(k == s)
            def _():
                reduce_step(0, s, nrs_ref)

        put(k, 1, solve(G[K + k].reshape(NB, W) - T[k], 1), sf_ref)

        @pl.when(k >= 1)
        def _():
            trail(k - 1)

    reduce_step(1, 0, nrf_ref)
    trail(K - 1)
    reduce_step(1, 1, nrf_ref)

    @pl.loop(0, N)
    def _(g):
        for s in range(4):
            for t in range(2):
                for d in range(2):
                    hop(g, t, s, d, False).wait_send()

    reduce_step(1, 2, nrf_ref)

    @pl.loop(0, K)
    def _(k):
        store(k).wait()

    reduce_step(1, 3, nrf_ref)
    for panel in range(2):
        for s in range(3):
            for copy in reduce_copies(panel, s):
                copy.wait_send()


def on_device(
    trail_rows, rows_first, rows_second, diag_first, diag_second, sub_block,
    cot_first, cot_second, cot_trail, cot_rows_first, cot_rows_second,
):
    rows, cols = trail_rows.shape
    K = rows // W
    shape = jax.ShapeDtypeStruct
    hbm = pl.BlockSpec(memory_space=pl.ANY)
    vmem = pl.BlockSpec(memory_space=pltpu.VMEM)
    dma = pltpu.SemaphoreType.DMA
    new_trail, new_first, new_second, first_t, second_t = pl.pallas_call(
        kernel,
        out_shape=(
            shape((rows, cols), F32),
            shape((64, cols), F32),
            shape((64, cols), F32),
            shape((32, rows), F32),
            shape((32, rows), F32),
        ),
        in_specs=[hbm] * 11,
        out_specs=(hbm, vmem, vmem, vmem, vmem),
        scratch_shapes=[
            pltpu.VMEM((2 * K, 4, 4, 32, W), F32),
            pltpu.VMEM((K, NB, W), F32),
            pltpu.VMEM((K, 2 * NB, W), BF),
            pltpu.VMEM((rows, cols), F32),
            pltpu.VMEM((rows, cols), BF),
            pltpu.VMEM((2 * NB, cols), BF),
            pltpu.VMEM((2, NB, NB), F32),
            pltpu.VMEM((NB, NB), F32),
            pltpu.VMEM((2, NB, cols), F32),
            pltpu.VMEM((2, 4, 64, cols), F32),
            pltpu.VMEM((2, 2, 4, 64, cols), F32),
            pltpu.VMEM((2, 2, 32, cols), F32),
            pltpu.VMEM((2, 2, 64, cols), F32),
            pltpu.VMEM((2, 64, cols), F32),
            pltpu.VMEM((NB, W), F32),
            pltpu.VMEM((4, NB, HALF), BF),
            pltpu.VMEM((2, NB, HALF), BF),
            pltpu.VMEM((2 * NB, NB), BF),
            dma((2 * K,)),
            dma((9,)),
            dma((K,)),
            dma((2 * K, 16)),
            dma((2 * K, 16)),
            dma((10,)),
            dma((10,)),
        ],
        compiler_params=pltpu.CompilerParams(
            collective_id=0, has_side_effects=True, vmem_limit_bytes=62 * 1024 * 1024
        ),
    )(
        cot_second.T, cot_first.T, trail_rows, rows_second, rows_first, diag_second, diag_first,
        sub_block, cot_trail, cot_rows_first, cot_rows_second,
    )
    return new_trail, new_first, new_second, first_t.T, second_t.T


def solution(mesh):
    both = P("row", "col")
    col = P(None, "col")
    return jax.shard_map(
        on_device,
        mesh=mesh,
        in_specs=(both, col, col, P(), P(), P(), both, both, both, both, both),
        out_specs=(both,) * 5,
        check_vma=False,
    )
```

```python
import functools

import jax
import jax.numpy as jnp
from jax import lax
from jax.experimental import pallas as pl
from jax.experimental.pallas import tpu as pltpu
from jax.sharding import PartitionSpec as P

MESH = pl.DeviceIdType.MESH
BF = jnp.bfloat16
F32 = jnp.float32
W = 512
LEAD = (8, 6, 3, 1, 0)
FILL = (
    ((0, 0), (1, 0), (2, 0), (3, 0)),
    ((0, 1), (1, 1), (4, 0), (5, 0)),
    ((0, 2), (2, 1), (3, 1), (6, 0)),
    ((1, 2), (4, 1), (7, 0)),
    ((0, 3), (2, 2), (5, 1)),
)
NB = 512
HALF = NB // 2


def split(value):
    high = value.astype(BF)
    return high, (value - high.astype(F32)).astype(BF)


def dot(left, right):
    return jnp.dot(left, right, preferred_element_type=F32)


def dot3(left, right):
    lh, ll = left
    rh, rl = right
    return dot(lh, rh) + (dot(lh, rl) + dot(ll, rh))


def dot_tall(stacked, right):
    rh, rl = right
    rows = stacked.shape[0] // 2
    both = dot(stacked, rh)
    return both[:rows] + (both[rows:] + dot(stacked[:rows], rl))


def invert_lower(blocks):
    base, groups = 32, 4
    parts = 2 * len(blocks)
    shape = (base * parts, 128)
    row = lax.rem(lax.broadcasted_iota(jnp.int32, shape, 0), base)
    lane = lax.broadcasted_iota(jnp.int32, shape, 1)
    first = lane // base * base
    group = lane[:base] // base
    packs = []
    for block in blocks:
        for h in range(2):
            part = block[128 * h : 128 * h + 128, 128 * h : 128 * h + 128]
            pack = part[:base]
            for q in range(1, groups):
                pack = jnp.where(group == q, part[base * q : base * q + base], pack)
            packs.append(pack)
    pack = jnp.concatenate(packs, axis=0)
    on_diag = row == lane - first
    diag_cols = jnp.where(on_diag, pack, 0.0)
    diag_rows = jnp.take_along_axis(pack, first + row, axis=1)
    unit = jnp.where(lane - first < row, pack / diag_rows, 0.0)
    inv = jnp.where(on_diag, 1.0, 0.0).astype(F32)
    for k in range(base - 1):
        column = jnp.take_along_axis(unit, first + k, axis=1)
        pivot = jnp.concatenate(
            [jnp.broadcast_to(inv[k + base * h : k + base * h + 1], (base, 128)) for h in range(parts)], axis=0
        )
        inv = inv - column * pivot
    results = []
    zero = jnp.zeros((128, 128), F32)
    for i in range(len(blocks)):
        pieces = []
        for h in range(2):
            mine = slice(base * (2 * i + h), base * (2 * i + h) + base)
            scaled = inv[mine] / jnp.sum(diag_cols[mine], axis=0, keepdims=True)
            full = jnp.concatenate([jnp.where(group == q, scaled, 0.0) for q in range(groups)], axis=0)
            pieces.append(jnp.concatenate([full, zero] if h == 0 else [zero, full], axis=1))
        results.append(jnp.concatenate(pieces, axis=0))
    brow = lax.broadcasted_iota(jnp.int32, (HALF, HALF), 0)
    bcol = lax.broadcasted_iota(jnp.int32, (HALF, HALF), 1)
    for size in (32, 64, 128):
        below = (brow // size == bcol // size + 1) & (lax.rem(bcol // size, 2) == 0)
        halves = [split(result) for result in results]
        inner = [dot3(split(jnp.where(below, b, 0.0)), h) for b, h in zip(blocks, halves)]
        outer = [dot3(h, split(v)) for h, v in zip(halves, inner)]
        results = [result - v for result, v in zip(results, outer)]
    return results


def kernel(
    cs_ref, cf_ref, trail_ref, rs_ref, rf_ref, ds_ref, df_ref, e_ref, ct_ref, crf_ref, crs_ref,
    CT, nrf_ref, nrs_ref, sf_ref, ss_ref,
    G, T, L, TR, R, D, E, acc, XB, PB, HB, FB, CR, inv_s, off_s, e_s,
    lsem, isem, ssem, rsem, rs_send, rs_recv,
):
    K = G.shape[0] // 2
    N = 2 * K
    c = lax.axis_index("col")
    r = lax.axis_index("row")
    x, z = c // 4, lax.rem(c, 4)
    y, core = r // 2, lax.rem(r, 2)
    x_p, x_m = lax.rem(x + 1, 4), lax.rem(x + 3, 4)
    z_p, z_m = lax.rem(z + 1, 4), lax.rem(z + 3, 4)
    y_p, y_m = lax.rem(y + 1, 4), lax.rem(y + 3, 4)
    to = (
        ({"col": x_p * 4 + z, "row": r}, {"col": x_m * 4 + z, "row": r}),
        ({"col": x * 4 + z_p, "row": r}, {"col": x * 4 + z_m, "row": r}),
        ({"col": c, "row": 2 * y_p + core}, {"col": c, "row": 2 * y_m + core}),
    )
    other = {"col": c, "row": 2 * y + 1 - core}

    def own(g, source):
        k = lax.rem(g, K)
        lanes = pl.ds(pl.multiple_of(k * W, 128), W)
        return pltpu.make_async_copy(source.at[:, lanes], G.at[g, x, z], lsem.at[g])

    @pl.loop(0, K)
    def _(k):
        own(k, cs_ref).start()

    @pl.loop(0, K)
    def _(k):
        own(k + K, cf_ref).start()

    loads = [
        pltpu.make_async_copy(ds_ref, D.at[0], isem.at[0]),
        pltpu.make_async_copy(df_ref, D.at[1], isem.at[1]),
        pltpu.make_async_copy(e_ref, E, isem.at[2]),
        pltpu.make_async_copy(trail_ref, TR, isem.at[3]),
        pltpu.make_async_copy(rs_ref, R.at[:NB], isem.at[4]),
        pltpu.make_async_copy(rf_ref, R.at[NB:], isem.at[5]),
        pltpu.make_async_copy(crs_ref, CR.at[0], isem.at[6]),
        pltpu.make_async_copy(crf_ref, CR.at[1], isem.at[7]),
        pltpu.make_async_copy(ct_ref, CT, isem.at[8]),
    ]
    for load in loads:
        load.start()

    barrier = pltpu.get_barrier_semaphore()
    for pair in to:
        for device in pair:
            pl.semaphore_signal(barrier, 1, device_id=device, device_id_type=MESH)
    pl.semaphore_signal(barrier, 1, device_id=other, device_id_type=MESH)
    pl.semaphore_wait(barrier, 7)

    def hop(g, t, s, d, landing):
        i1, m1, p1 = ((x, x_m, x_p), (z, z_m, z_p))[t]
        i2, m2, p2 = ((z, z_m, z_p), (x, x_m, x_p))[t]
        near = lambda mine, minus, plus: (minus if d == 0 else plus)
        opposite = lambda mine: lax.rem(mine + 2, 4)
        rows, half = pl.ds(16 * t, 16), pl.ds(16 * t + 8 * d, 8)
        every = slice(None)
        if s == 0:
            a, b, part = (near(i1, m1, p1) if landing else i1), i2, rows
        elif s == 1:
            a, b, part = (opposite(i1) if landing else near(i1, m1, p1)), i2, half
        elif s == 2:
            a, b, part = every, (near(i2, m2, p2) if landing else i2), rows
        else:
            a, b, part = every, (opposite(i2) if landing else near(i2, m2, p2)), half
        ref = G.at[g, a, b, part] if t == 0 else G.at[g, b, a, part]
        axis = t if s < 2 else 1 - t
        index = t * 8 + s * 2 + d
        return pltpu.make_async_remote_copy(
            ref, ref, ssem.at[g, index], rsem.at[g, index], device_id=to[axis][d], device_id_type=MESH
        )

    def stage(g, s):
        if s == 0:
            own(g, cs_ref).wait()
        else:
            for t in range(2):
                for d in range(2):
                    hop(g, t, s - 1, d, True).wait_recv()
        if s < 4:
            for t in range(2):
                for d in range(2):
                    hop(g, t, s, d, False).start()

    def communicate(n):
        for s in (3, 2, 1, 0, 4):
            g = n + LEAD[s]

            @pl.when(g < N)
            def _():
                stage(g, s)

    def invert(panel):
        loads[panel].wait()
        blocks = [D[panel, HALF * i : HALF * i + HALF, HALF * i : HALF * i + HALF] for i in range(2)]
        for i, inverse in enumerate(invert_lower(blocks)):
            high, low = split(inverse.T)
            inv_s[2 * panel + i, :HALF] = high
            inv_s[2 * panel + i, HALF:] = low
        high, low = split(D[panel, HALF:, :HALF].T)
        off_s[panel, :HALF] = high
        off_s[panel, HALF:] = low

    def transpose_sub():
        loads[2].wait()
        high, low = split(E[...].T)
        e_s[:NB] = high
        e_s[NB:] = low
        acc[...] = jnp.zeros_like(acc)

    pieces = {1: functools.partial(invert, 0), 2: functools.partial(invert, 1), 3: transpose_sub}
    for i, hops in enumerate(FILL):
        for g, s in hops:
            stage(g, s)
        if i in pieces:
            pieces[i]()
    for load in loads[3:]:
        load.wait()

    def solve(right, panel):
        x1 = dot_tall(inv_s[2 * panel + 1], split(right[HALF:]))
        x1_parts = split(x1)
        left = right[:HALF] - dot_tall(off_s[panel], x1_parts)
        x0 = dot_tall(inv_s[2 * panel], split(left))
        return x0, x1, split(x0), x1_parts

    def put(k, panel, solved, out_ref):
        x0, x1, (h0, _), (h1, _) = solved
        lanes = pl.ds(pl.multiple_of(k * W, 128), W)
        for i in range(16):

            @pl.when(c == i)
            def _():
                out_ref[:, lanes] = (x0, x1)[i // 8][32 * (i % 8) : 32 * (i % 8) + 32]

        L[:HALF] = h0
        L[HALF:] = h1
        rows = TR[pl.ds(pl.multiple_of(k * W, 128), W)]
        for q in range(2):
            acc[panel, 2 * q : 2 * q + 2] += dot((h0, h1)[q], rows).reshape(2, 2, 64, rows.shape[1])

    far = lax.rem(y + 2, 4)

    def reduce_copies(panel, first, last):
        part = lambda buffer, i, rows: buffer.at[panel, i, rows]
        top, low, to_p, to_m = pl.ds(0, 32), pl.ds(32, 32), to[2][0], to[2][1]
        moves = [(acc.at[panel, q, 1 - core], XB.at[panel, q], other) for q in (far, y_p, y_m, y)] + [
            (part(PB, far, top), HB.at[panel, 0], to_p),
            (part(PB, far, low), HB.at[panel, 1], to_m),
            (part(PB, y_p, low), part(FB, 0, low), to_p),
            (part(PB, y_m, top), part(FB, 1, top), to_m),
            (part(PB, y_p, top), part(FB, 0, top), to_p),
            (part(PB, y_m, low), part(FB, 1, low), to_m),
        ]
        return [
            pltpu.make_async_remote_copy(
                src, dst, rs_send.at[panel, i], rs_recv.at[panel, i], device_id=device, device_id_type=MESH
            )
            for i, (src, dst, device) in list(enumerate(moves))[first:last]
        ]

    def start(panel, first, last):
        for copy in reduce_copies(panel, first, last):
            copy.start()

    def arrive(panel, first, last):
        for copy in reduce_copies(panel, first, last):
            copy.wait_recv()

    def reduce_step(panel, s, out_ref):
        if s == 0:
            start(panel, 0, 4)
        elif s == 1:
            for i, q in enumerate((far, y_p, y_m, y)):
                arrive(panel, i, i + 1)
                PB[panel, q] = acc[panel, q, core] + XB[panel, q]
                if i == 0:
                    start(panel, 4, 6)
                elif i < 3:
                    start(panel, 5 + i, 6 + i)
        elif s == 2:
            arrive(panel, 4, 6)
            PB[panel, y_p, :32] += HB[panel, 0]
            PB[panel, y_m, 32:] += HB[panel, 1]
            start(panel, 8, 10)
        else:
            arrive(panel, 6, 10)
            out_ref[...] = CR[panel] - ((PB[panel, y] + FB[panel, 0]) + FB[panel, 1])

    def trail(k, panel):
        rows = pl.ds(pl.multiple_of(k * W, W), W)
        right = R[NB * panel : NB * panel + NB]
        update = lax.dot_general(L[...], right, (((0,), (0,)), ((), ())), preferred_element_type=F32)
        CT[rows] -= update

    @pl.loop(0, K)
    def _(k):
        communicate(k)
        solved = solve(G[k].reshape(NB, W), 0)
        put(k, 0, solved, ss_ref)
        trail(k, 0)
        T[k] = dot_tall(e_s[...], tuple(jnp.concatenate(p, axis=0) for p in zip(solved[2], solved[3])))

    @pl.loop(0, K)
    def _(k):
        communicate(K + k)
        for s in range(4):

            @pl.when(k == s)
            def _():
                reduce_step(0, s, nrs_ref)

        @pl.when(k >= 1)
        def _():
            trail(k - 1, 1)

        put(k, 1, solve(G[K + k].reshape(NB, W) - T[k], 1), sf_ref)

    reduce_step(1, 0, nrf_ref)
    trail(K - 1, 1)
    reduce_step(1, 1, nrf_ref)

    @pl.loop(0, N)
    def _(g):
        for s in range(4):
            for t in range(2):
                for d in range(2):
                    hop(g, t, s, d, False).wait_send()

    reduce_step(1, 2, nrf_ref)

    reduce_step(1, 3, nrf_ref)
    for panel in range(2):
        for copy in reduce_copies(panel, 0, 10):
            copy.wait_send()


def on_device(
    trail_rows, rows_first, rows_second, diag_first, diag_second, sub_block,
    cot_first, cot_second, cot_trail, cot_rows_first, cot_rows_second,
):
    rows, cols = trail_rows.shape
    K = rows // W
    shape = jax.ShapeDtypeStruct
    hbm = pl.BlockSpec(memory_space=pl.ANY)
    vmem = pl.BlockSpec(memory_space=pltpu.VMEM)
    dma = pltpu.SemaphoreType.DMA
    results = pl.pallas_call(
        kernel,
        out_shape=(
            pltpu.VMEM((rows, cols), F32),
            pltpu.VMEM((64, cols), F32),
            pltpu.VMEM((64, cols), F32),
            pltpu.VMEM((32, rows), F32),
            pltpu.VMEM((32, rows), F32),
        ),
        in_specs=[hbm] * 11,
        out_specs=(vmem,) * 5,
        scratch_shapes=[
            pltpu.VMEM((2 * K, 4, 4, 32, W), F32),
            pltpu.VMEM((K, NB, W), F32),
            pltpu.VMEM((NB, W), BF),
            pltpu.VMEM((rows, cols), BF),
            pltpu.VMEM((2 * NB, cols), BF),
            pltpu.VMEM((2, NB, NB), F32),
            pltpu.VMEM((NB, NB), F32),
            pltpu.VMEM((2, 4, 2, 64, cols), F32),
            pltpu.VMEM((2, 4, 64, cols), F32),
            pltpu.VMEM((2, 4, 64, cols), F32),
            pltpu.VMEM((2, 2, 32, cols), F32),
            pltpu.VMEM((2, 2, 64, cols), F32),
            pltpu.VMEM((2, 64, cols), F32),
            pltpu.VMEM((4, NB, HALF), BF),
            pltpu.VMEM((2, NB, HALF), BF),
            pltpu.VMEM((2 * NB, NB), BF),
            dma((2 * K,)),
            dma((9,)),
            dma((2 * K, 16)),
            dma((2 * K, 16)),
            dma((2, 10)),
            dma((2, 10)),
        ],
        compiler_params=pltpu.CompilerParams(
            collective_id=0, has_side_effects=True, vmem_limit_bytes=50 * 1024 * 1024
        ),
    )(
        cot_second.T, cot_first.T, trail_rows, rows_second, rows_first, diag_second, diag_first,
        sub_block, cot_trail, cot_rows_first, cot_rows_second,
    )
    new_trail, new_first, new_second, first_t, second_t = results
    return new_trail, new_first, new_second, first_t.T, second_t.T


def solution(mesh):
    both = P("row", "col")
    col = P(None, "col")
    return jax.shard_map(
        on_device,
        mesh=mesh,
        in_specs=(both, col, col, P(), P(), P(), both, both, both, both, both),
        out_specs=(both,) * 5,
        check_vma=False,
    )
```

```python
import functools

import jax
import jax.numpy as jnp
from jax import lax
from jax.experimental import pallas as pl
from jax.experimental.pallas import tpu as pltpu
from jax.sharding import PartitionSpec as P

MESH = pl.DeviceIdType.MESH
BF = jnp.bfloat16
F32 = jnp.float32
W = 512
LEAD = (8, 6, 3, 1, 0)
FILL = (
    ((0, 0), (1, 0), (2, 0), (3, 0)),
    ((0, 1), (1, 1), (4, 0), (5, 0)),
    ((0, 2), (2, 1), (3, 1), (6, 0)),
    ((1, 2), (4, 1), (7, 0)),
    ((0, 3), (2, 2), (5, 1)),
)
NB = 512
HALF = NB // 2


def split(value):
    high = value.astype(BF)
    return high, (value - high.astype(F32)).astype(BF)


def dot(left, right):
    return jnp.dot(left, right, preferred_element_type=F32)


def dot3(left, right):
    lh, ll = left
    rh, rl = right
    return dot(lh, rh) + (dot(lh, rl) + dot(ll, rh))


def dot_tall(stacked, right):
    rh, rl = right
    rows = stacked.shape[0] // 2
    both = dot(stacked, rh)
    return both[:rows] + (both[rows:] + dot(stacked[:rows], rl))


def invert_lower(blocks):
    base, groups = 32, 4
    parts = 2 * len(blocks)
    shape = (base * parts, 128)
    row = lax.rem(lax.broadcasted_iota(jnp.int32, shape, 0), base)
    lane = lax.broadcasted_iota(jnp.int32, shape, 1)
    first = lane // base * base
    group = lane[:base] // base
    packs = []
    for block in blocks:
        for h in range(2):
            part = block[128 * h : 128 * h + 128, 128 * h : 128 * h + 128]
            pack = part[:base]
            for q in range(1, groups):
                pack = jnp.where(group == q, part[base * q : base * q + base], pack)
            packs.append(pack)
    pack = jnp.concatenate(packs, axis=0)
    on_diag = row == lane - first
    diag_cols = jnp.where(on_diag, pack, 0.0)
    diag_rows = jnp.take_along_axis(pack, first + row, axis=1)
    unit = jnp.where(lane - first < row, pack / diag_rows, 0.0)
    inv = jnp.where(on_diag, 1.0, 0.0).astype(F32)
    for k in range(base - 1):
        column = jnp.take_along_axis(unit, first + k, axis=1)
        pivot = jnp.concatenate(
            [jnp.broadcast_to(inv[k + base * h : k + base * h + 1], (base, 128)) for h in range(parts)], axis=0
        )
        inv = inv - column * pivot
    results = []
    zero = jnp.zeros((128, 128), F32)
    for i in range(len(blocks)):
        pieces = []
        for h in range(2):
            mine = slice(base * (2 * i + h), base * (2 * i + h) + base)
            scaled = inv[mine] / jnp.sum(diag_cols[mine], axis=0, keepdims=True)
            full = jnp.concatenate([jnp.where(group == q, scaled, 0.0) for q in range(groups)], axis=0)
            pieces.append(jnp.concatenate([full, zero] if h == 0 else [zero, full], axis=1))
        results.append(jnp.concatenate(pieces, axis=0))
    brow = lax.broadcasted_iota(jnp.int32, (HALF, HALF), 0)
    bcol = lax.broadcasted_iota(jnp.int32, (HALF, HALF), 1)
    for size in (32, 64, 128):
        below = (brow // size == bcol // size + 1) & (lax.rem(bcol // size, 2) == 0)
        halves = [split(result) for result in results]
        inner = [dot3(split(jnp.where(below, b, 0.0)), h) for b, h in zip(blocks, halves)]
        outer = [dot3(h, split(v)) for h, v in zip(halves, inner)]
        results = [result - v for result, v in zip(results, outer)]
    return results


def kernel(
    cs_ref, cf_ref, trail_ref, rs_ref, rf_ref, ds_ref, df_ref, e_ref, ct_ref, crf_ref, crs_ref,
    CT, n_ref, s_ref,
    G, T, L, TR, R, D, E, acc, XB, PB, HB, FB, CR, inv_s, off_s, e_s,
    lsem, isem, ssem, rsem, rs_send, rs_recv,
):
    K = G.shape[0] // 2
    nrf_ref, nrs_ref, sf_ref, ss_ref = n_ref.at[0], n_ref.at[1], s_ref.at[0], s_ref.at[1]
    N = 2 * K
    c = lax.axis_index("col")
    r = lax.axis_index("row")
    x, z = c // 4, lax.rem(c, 4)
    y, core = r // 2, lax.rem(r, 2)
    x_p, x_m = lax.rem(x + 1, 4), lax.rem(x + 3, 4)
    z_p, z_m = lax.rem(z + 1, 4), lax.rem(z + 3, 4)
    y_p, y_m = lax.rem(y + 1, 4), lax.rem(y + 3, 4)
    to = (
        ({"col": x_p * 4 + z, "row": r}, {"col": x_m * 4 + z, "row": r}),
        ({"col": x * 4 + z_p, "row": r}, {"col": x * 4 + z_m, "row": r}),
        ({"col": c, "row": 2 * y_p + core}, {"col": c, "row": 2 * y_m + core}),
    )
    other = {"col": c, "row": 2 * y + 1 - core}

    def own(g, source):
        k = lax.rem(g, K)
        lanes = pl.ds(pl.multiple_of(k * W, 128), W)
        return pltpu.make_async_copy(source.at[:, lanes], G.at[g, x, z], lsem.at[g])

    @pl.loop(0, K)
    def _(k):
        own(k, cs_ref).start()

    @pl.loop(0, K)
    def _(k):
        own(k + K, cf_ref).start()

    loads = [
        pltpu.make_async_copy(ds_ref, D.at[0], isem.at[0]),
        pltpu.make_async_copy(df_ref, D.at[1], isem.at[1]),
        pltpu.make_async_copy(e_ref, E, isem.at[2]),
        pltpu.make_async_copy(trail_ref, TR, isem.at[3]),
        pltpu.make_async_copy(rs_ref, R.at[:NB], isem.at[4]),
        pltpu.make_async_copy(rf_ref, R.at[NB:], isem.at[5]),
        pltpu.make_async_copy(crs_ref, CR.at[0], isem.at[6]),
        pltpu.make_async_copy(crf_ref, CR.at[1], isem.at[7]),
        pltpu.make_async_copy(ct_ref, CT, isem.at[8]),
    ]
    for load in loads:
        load.start()

    barrier = pltpu.get_barrier_semaphore()
    for pair in to:
        for device in pair:
            pl.semaphore_signal(barrier, 1, device_id=device, device_id_type=MESH)
    pl.semaphore_signal(barrier, 1, device_id=other, device_id_type=MESH)
    pl.semaphore_wait(barrier, 7)

    def hop(g, t, s, d, landing):
        i1, m1, p1 = ((x, x_m, x_p), (z, z_m, z_p))[t]
        i2, m2, p2 = ((z, z_m, z_p), (x, x_m, x_p))[t]
        near = lambda mine, minus, plus: (minus if d == 0 else plus)
        opposite = lambda mine: lax.rem(mine + 2, 4)
        rows, half = pl.ds(16 * t, 16), pl.ds(16 * t + 8 * d, 8)
        every = slice(None)
        if s == 0:
            a, b, part = (near(i1, m1, p1) if landing else i1), i2, rows
        elif s == 1:
            a, b, part = (opposite(i1) if landing else near(i1, m1, p1)), i2, half
        elif s == 2:
            a, b, part = every, (near(i2, m2, p2) if landing else i2), rows
        else:
            a, b, part = every, (opposite(i2) if landing else near(i2, m2, p2)), half
        ref = G.at[g, a, b, part] if t == 0 else G.at[g, b, a, part]
        axis = t if s < 2 else 1 - t
        index = t * 8 + s * 2 + d
        return pltpu.make_async_remote_copy(
            ref, ref, ssem.at[g, index], rsem.at[g, index], device_id=to[axis][d], device_id_type=MESH
        )

    def stage(g, s):
        if s == 0:
            own(g, cs_ref).wait()
        else:
            for t in range(2):
                for d in range(2):
                    hop(g, t, s - 1, d, True).wait_recv()
        if s < 4:
            for t in range(2):
                for d in range(2):
                    hop(g, t, s, d, False).start()

    def communicate(n, hops):
        for s in hops:
            g = n + LEAD[s]

            @pl.when(g < N)
            def _():
                stage(g, s)

    def invert(panel):
        loads[panel].wait()
        blocks = [D[panel, HALF * i : HALF * i + HALF, HALF * i : HALF * i + HALF] for i in range(2)]
        for i, inverse in enumerate(invert_lower(blocks)):
            high, low = split(inverse.T)
            inv_s[2 * panel + i, :HALF] = high
            inv_s[2 * panel + i, HALF:] = low
        high, low = split(D[panel, HALF:, :HALF].T)
        off_s[panel, :HALF] = high
        off_s[panel, HALF:] = low

    def transpose_sub():
        loads[2].wait()
        high, low = split(E[...].T)
        e_s[:NB] = high
        e_s[NB:] = low
        acc[...] = jnp.zeros_like(acc)

    pieces = {1: functools.partial(invert, 0), 2: functools.partial(invert, 1), 3: transpose_sub}
    for i, hops in enumerate(FILL):
        for g, s in hops:
            stage(g, s)
        if i in pieces:
            pieces[i]()
    for load in loads[3:]:
        load.wait()

    def solve_part(right, panel, q):
        x = dot_tall(inv_s[2 * panel + q], split(right))
        return x, split(x)

    def add_product(k, panel, q, high):
        rows = TR[pl.ds(pl.multiple_of(k * W, 128), W)]
        acc[panel, 2 * q : 2 * q + 2] += dot(high, rows).reshape(2, 2, 64, rows.shape[1])

    def chunk(k, panel, right, out_ref, after=lambda q: None):
        x1, parts1 = solve_part(right[HALF:], panel, 1)
        L[HALF:] = parts1[0]
        add_product(k, panel, 1, parts1[0])
        after(1)
        x0, parts0 = solve_part(right[:HALF] - dot_tall(off_s[panel], parts1), panel, 0)
        L[:HALF] = parts0[0]
        add_product(k, panel, 0, parts0[0])
        after(0)
        lanes = pl.ds(pl.multiple_of(k * W, 128), W)
        for i in range(16):

            @pl.when(c == i)
            def _():
                out_ref[:, lanes] = (x0, x1)[i // 8][32 * (i % 8) : 32 * (i % 8) + 32]

        return parts0, parts1

    far = lax.rem(y + 2, 4)

    def reduce_copies(panel, first, last):
        part = lambda buffer, i, rows: buffer.at[panel, i, rows]
        top, low, to_p, to_m = pl.ds(0, 32), pl.ds(32, 32), to[2][0], to[2][1]
        moves = [(acc.at[panel, q, 1 - core], XB.at[panel, q], other) for q in range(4)] + [
            (part(PB, far, top), HB.at[panel, 0], to_p),
            (part(PB, far, low), HB.at[panel, 1], to_m),
            (part(PB, y_p, low), part(FB, 0, low), to_p),
            (part(PB, y_m, top), part(FB, 1, top), to_m),
            (part(PB, y_p, top), part(FB, 0, top), to_p),
            (part(PB, y_m, low), part(FB, 1, low), to_m),
        ]
        return [
            pltpu.make_async_remote_copy(
                src, dst, rs_send.at[panel, i], rs_recv.at[panel, i], device_id=device, device_id_type=MESH
            )
            for i, (src, dst, device) in list(enumerate(moves))[first:last]
        ]

    def start(panel, first, last):
        for copy in reduce_copies(panel, first, last):
            copy.start()

    def arrive(panel, first, last):
        for copy in reduce_copies(panel, first, last):
            copy.wait_recv()

    def reduce_step(panel, s, out_ref):
        if s == 0:
            start(panel, 0, 4)
        elif s == 1:
            for i, q in enumerate((far, y_p, y_m, y)):
                pltpu.make_async_remote_copy(
                    acc.at[panel, q, 1 - core], XB.at[panel, q], rs_send.at[panel, q], rs_recv.at[panel, q],
                    device_id=other, device_id_type=MESH,
                ).wait_recv()
                PB[panel, q] = acc[panel, q, core] + XB[panel, q]
                if i == 0:
                    start(panel, 4, 6)
                elif i < 3:
                    start(panel, 5 + i, 6 + i)
        elif s == 2:
            arrive(panel, 4, 6)
            PB[panel, y_p, :32] += HB[panel, 0]
            PB[panel, y_m, 32:] += HB[panel, 1]
            start(panel, 8, 10)
        else:
            arrive(panel, 6, 10)
            out_ref[...] = CR[panel] - ((PB[panel, y] + FB[panel, 0]) + FB[panel, 1])

    def trail(k, panel):
        rows = pl.ds(pl.multiple_of(k * W, W), W)
        right = R[NB * panel : NB * panel + NB]
        update = lax.dot_general(L[...], right, (((0,), (0,)), ((), ())), preferred_element_type=F32)
        CT[rows] -= update

    @pl.loop(0, K)
    def _(k):
        communicate(k, (3, 2, 1, 0, 4))
        parts = chunk(k, 0, G[k].reshape(NB, W), ss_ref)
        trail(k, 0)
        T[k] = dot_tall(e_s[...], tuple(jnp.concatenate(p, axis=0) for p in zip(*parts)))

    @pl.loop(0, K - 1)
    def _(k):
        communicate(K + k, (3, 2, 1, 0))
        for s in range(4):

            @pl.when(k == s)
            def _():
                reduce_step(0, s, nrs_ref)

        @pl.when(k >= 1)
        def _():
            trail(k - 1, 1)

        communicate(K + k, (4,))
        chunk(k, 1, G[K + k].reshape(NB, W) - T[k], sf_ref)

    trail(K - 2, 1)
    stage(N - 1, 4)
    chunk(K - 1, 1, G[N - 1].reshape(NB, W) - T[K - 1], sf_ref, lambda q: start(1, 2 * q, 2 * q + 2))
    trail(K - 1, 1)
    reduce_step(1, 1, nrf_ref)

    @pl.loop(0, N)
    def _(g):
        for s in range(4):
            for t in range(2):
                for d in range(2):
                    hop(g, t, s, d, False).wait_send()

    reduce_step(1, 2, nrf_ref)

    reduce_step(1, 3, nrf_ref)
    for panel in range(2):
        for copy in reduce_copies(panel, 0, 10):
            copy.wait_send()


def on_device(
    trail_rows, rows_first, rows_second, diag_first, diag_second, sub_block,
    cot_first, cot_second, cot_trail, cot_rows_first, cot_rows_second,
):
    rows, cols = trail_rows.shape
    K = rows // W
    shape = jax.ShapeDtypeStruct
    hbm = pl.BlockSpec(memory_space=pl.ANY)
    vmem = pl.BlockSpec(memory_space=pltpu.VMEM)
    dma = pltpu.SemaphoreType.DMA
    results = pl.pallas_call(
        kernel,
        out_shape=(
            pltpu.VMEM((rows, cols), F32),
            pltpu.VMEM((2, 64, cols), F32),
            pltpu.VMEM((2, 32, rows), F32),
        ),
        in_specs=[hbm] * 11,
        out_specs=(vmem,) * 3,
        scratch_shapes=[
            pltpu.VMEM((2 * K, 4, 4, 32, W), F32),
            pltpu.VMEM((K, NB, W), F32),
            pltpu.VMEM((NB, W), BF),
            pltpu.VMEM((rows, cols), BF),
            pltpu.VMEM((2 * NB, cols), BF),
            pltpu.VMEM((2, NB, NB), F32),
            pltpu.VMEM((NB, NB), F32),
            pltpu.VMEM((2, 4, 2, 64, cols), F32),
            pltpu.VMEM((2, 4, 64, cols), F32),
            pltpu.VMEM((2, 4, 64, cols), F32),
            pltpu.VMEM((2, 2, 32, cols), F32),
            pltpu.VMEM((2, 2, 64, cols), F32),
            pltpu.VMEM((2, 64, cols), F32),
            pltpu.VMEM((4, NB, HALF), BF),
            pltpu.VMEM((2, NB, HALF), BF),
            pltpu.VMEM((2 * NB, NB), BF),
            dma((2 * K,)),
            dma((9,)),
            dma((2 * K, 16)),
            dma((2 * K, 16)),
            dma((2, 10)),
            dma((2, 10)),
        ],
        compiler_params=pltpu.CompilerParams(
            collective_id=0, has_side_effects=True, vmem_limit_bytes=50 * 1024 * 1024
        ),
    )(
        cot_second.T, cot_first.T, trail_rows, rows_second, rows_first, diag_second, diag_first,
        sub_block, cot_trail, cot_rows_first, cot_rows_second,
    )
    new_trail, (new_first, new_second), (first_t, second_t) = results[0], results[1], results[2]
    return new_trail, new_first, new_second, first_t.T, second_t.T


def solution(mesh):
    both = P("row", "col")
    col = P(None, "col")
    return jax.shard_map(
        on_device,
        mesh=mesh,
        in_specs=(both, col, col, P(), P(), P(), both, both, both, both, both),
        out_specs=(both,) * 5,
        check_vma=False,
    )
```

```python
import functools

import jax
import jax.numpy as jnp
from jax import lax
from jax.experimental import pallas as pl
from jax.experimental.pallas import tpu as pltpu
from jax.sharding import PartitionSpec as P

MESH = pl.DeviceIdType.MESH
BF = jnp.bfloat16
F32 = jnp.float32
W = 512
LEAD = (8, 6, 3, 1, 0)
FILL = (
    ((0, 0), (1, 0), (2, 0), (3, 0)),
    ((0, 1), (1, 1), (4, 0), (5, 0)),
    ((0, 2), (2, 1), (3, 1), (6, 0)),
    ((1, 2), (4, 1), (7, 0)),
    ((0, 3), (2, 2), (5, 1)),
)
NB = 512
HALF = NB // 2


def split(value):
    high = value.astype(BF)
    return high, (value - high.astype(F32)).astype(BF)


def dot(left, right):
    return jnp.dot(left, right, preferred_element_type=F32)


def dot3(left, right):
    lh, ll = left
    rh, rl = right
    return dot(lh, rh) + (dot(lh, rl) + dot(ll, rh))


def dot_tall(stacked, right):
    rh, rl = right
    rows = stacked.shape[0] // 2
    both = dot(stacked, rh)
    return both[:rows] + (both[rows:] + dot(stacked[:rows], rl))


def invert_lower(blocks):
    base, groups = 32, 4
    parts = 2 * len(blocks)
    shape = (base * parts, 128)
    row = lax.rem(lax.broadcasted_iota(jnp.int32, shape, 0), base)
    lane = lax.broadcasted_iota(jnp.int32, shape, 1)
    first = lane // base * base
    group = lane[:base] // base
    packs = []
    for block in blocks:
        for h in range(2):
            part = block[128 * h : 128 * h + 128, 128 * h : 128 * h + 128]
            pack = part[:base]
            for q in range(1, groups):
                pack = jnp.where(group == q, part[base * q : base * q + base], pack)
            packs.append(pack)
    pack = jnp.concatenate(packs, axis=0)
    on_diag = row == lane - first
    diag_cols = jnp.where(on_diag, pack, 0.0)
    diag_rows = jnp.take_along_axis(pack, first + row, axis=1)
    unit = jnp.where(lane - first < row, pack / diag_rows, 0.0)
    inv = jnp.where(on_diag, 1.0, 0.0).astype(F32)
    for k in range(base - 1):
        column = jnp.take_along_axis(unit, first + k, axis=1)
        pivot = jnp.concatenate(
            [jnp.broadcast_to(inv[k + base * h : k + base * h + 1], (base, 128)) for h in range(parts)], axis=0
        )
        inv = inv - column * pivot
    results = []
    zero = jnp.zeros((128, 128), F32)
    for i in range(len(blocks)):
        pieces = []
        for h in range(2):
            mine = slice(base * (2 * i + h), base * (2 * i + h) + base)
            scaled = inv[mine] / jnp.sum(diag_cols[mine], axis=0, keepdims=True)
            full = jnp.concatenate([jnp.where(group == q, scaled, 0.0) for q in range(groups)], axis=0)
            pieces.append(jnp.concatenate([full, zero] if h == 0 else [zero, full], axis=1))
        results.append(jnp.concatenate(pieces, axis=0))
    brow = lax.broadcasted_iota(jnp.int32, (HALF, HALF), 0)
    bcol = lax.broadcasted_iota(jnp.int32, (HALF, HALF), 1)
    for size in (32, 64, 128):
        below = (brow // size == bcol // size + 1) & (lax.rem(bcol // size, 2) == 0)
        halves = [split(result) for result in results]
        inner = [dot3(split(jnp.where(below, b, 0.0)), h) for b, h in zip(blocks, halves)]
        outer = [dot3(h, split(v)) for h, v in zip(halves, inner)]
        results = [result - v for result, v in zip(results, outer)]
    return results


def kernel(
    cs_ref, cf_ref, trail_ref, rs_ref, rf_ref, ds_ref, df_ref, e_ref, ct_ref, crf_ref, crs_ref,
    CT, n_ref, s_ref,
    G, T, L, TR, R, D, E, acc, XB, PB, HB, FB, CR, inv_s, off_s, e_s,
    lsem, isem, ssem, rsem, rs_send, rs_recv,
):
    K = G.shape[0] // 2
    nrf_ref, nrs_ref, sf_ref, ss_ref = n_ref.at[0], n_ref.at[1], s_ref.at[0], s_ref.at[1]
    N = 2 * K
    c = lax.axis_index("col")
    r = lax.axis_index("row")
    x, z = c // 4, lax.rem(c, 4)
    y, core = r // 2, lax.rem(r, 2)
    x_p, x_m = lax.rem(x + 1, 4), lax.rem(x + 3, 4)
    z_p, z_m = lax.rem(z + 1, 4), lax.rem(z + 3, 4)
    y_p, y_m = lax.rem(y + 1, 4), lax.rem(y + 3, 4)
    to = (
        ({"col": x_p * 4 + z, "row": r}, {"col": x_m * 4 + z, "row": r}),
        ({"col": x * 4 + z_p, "row": r}, {"col": x * 4 + z_m, "row": r}),
        ({"col": c, "row": 2 * y_p + core}, {"col": c, "row": 2 * y_m + core}),
    )
    other = {"col": c, "row": 2 * y + 1 - core}

    def own(g, source):
        k = lax.rem(g, K)
        lanes = pl.ds(pl.multiple_of(k * W, 128), W)
        return pltpu.make_async_copy(source.at[:, lanes], G.at[g, x, z], lsem.at[g])

    @pl.loop(0, K)
    def _(k):
        own(k, cs_ref).start()

    @pl.loop(0, K)
    def _(k):
        own(k + K, cf_ref).start()

    loads = [
        pltpu.make_async_copy(ds_ref, D.at[0], isem.at[0]),
        pltpu.make_async_copy(df_ref, D.at[1], isem.at[1]),
        pltpu.make_async_copy(e_ref, E, isem.at[2]),
        pltpu.make_async_copy(trail_ref, TR, isem.at[3]),
        pltpu.make_async_copy(rs_ref, R.at[:NB], isem.at[4]),
        pltpu.make_async_copy(rf_ref, R.at[NB:], isem.at[5]),
        pltpu.make_async_copy(crs_ref, CR.at[0], isem.at[6]),
        pltpu.make_async_copy(crf_ref, CR.at[1], isem.at[7]),
        pltpu.make_async_copy(ct_ref, CT, isem.at[8]),
    ]
    for load in loads:
        load.start()

    barrier = pltpu.get_barrier_semaphore()
    for pair in to:
        for device in pair:
            pl.semaphore_signal(barrier, 1, device_id=device, device_id_type=MESH)
    pl.semaphore_signal(barrier, 1, device_id=other, device_id_type=MESH)
    pl.semaphore_wait(barrier, 7)

    def hop(g, t, s, d, landing):
        i1, m1, p1 = ((x, x_m, x_p), (z, z_m, z_p))[t]
        i2, m2, p2 = ((z, z_m, z_p), (x, x_m, x_p))[t]
        near = lambda mine, minus, plus: (minus if d == 0 else plus)
        opposite = lambda mine: lax.rem(mine + 2, 4)
        rows, half = pl.ds(16 * t, 16), pl.ds(16 * t + 8 * d, 8)
        every = slice(None)
        if s == 0:
            a, b, part = (near(i1, m1, p1) if landing else i1), i2, rows
        elif s == 1:
            a, b, part = (opposite(i1) if landing else near(i1, m1, p1)), i2, half
        elif s == 2:
            a, b, part = every, (near(i2, m2, p2) if landing else i2), rows
        else:
            a, b, part = every, (opposite(i2) if landing else near(i2, m2, p2)), half
        ref = G.at[g, a, b, part] if t == 0 else G.at[g, b, a, part]
        axis = t if s < 2 else 1 - t
        index = t * 8 + s * 2 + d
        return pltpu.make_async_remote_copy(
            ref, ref, ssem.at[g, index], rsem.at[g, index], device_id=to[axis][d], device_id_type=MESH
        )

    def stage(g, s):
        if s == 0:
            own(g, cs_ref).wait()
        else:
            for t in range(2):
                for d in range(2):
                    hop(g, t, s - 1, d, True).wait_recv()
        if s < 4:
            for t in range(2):
                for d in range(2):
                    hop(g, t, s, d, False).start()

    def communicate(n, hops):
        for s in hops:
            g = n + LEAD[s]

            @pl.when(g < N)
            def _():
                stage(g, s)

    def invert(panel):
        loads[panel].wait()
        blocks = [D[panel, HALF * i : HALF * i + HALF, HALF * i : HALF * i + HALF] for i in range(2)]
        for i, inverse in enumerate(invert_lower(blocks)):
            high, low = split(inverse.T)
            inv_s[2 * panel + i, :HALF] = high
            inv_s[2 * panel + i, HALF:] = low
        high, low = split(D[panel, HALF:, :HALF].T)
        off_s[panel, :HALF] = high
        off_s[panel, HALF:] = low

    def transpose_sub():
        loads[2].wait()
        high, low = split(E[...].T)
        e_s[:NB] = high
        e_s[NB:] = low
        acc[...] = jnp.zeros_like(acc)

    pieces = {1: functools.partial(invert, 0), 2: functools.partial(invert, 1), 3: transpose_sub}
    for i, hops in enumerate(FILL):
        for g, s in hops:
            stage(g, s)
        if i in pieces:
            pieces[i]()
    for load in loads[3:]:
        load.wait()

    def solve_part(right, panel, q):
        x = dot_tall(inv_s[2 * panel + q], split(right))
        return x, split(x)

    def add_product(k, panel, q, high):
        rows = TR[pl.ds(pl.multiple_of(k * W, 128), W)]
        acc[panel, 2 * q : 2 * q + 2] += dot(high, rows).reshape(2, 2, 64, rows.shape[1])

    def chunk(k, panel, right, out_ref, after=lambda q: None):
        x1, parts1 = solve_part(right[HALF:], panel, 1)
        slot = lax.rem(k, 3)
        L[slot, HALF:] = parts1[0]
        add_product(k, panel, 1, parts1[0])
        after(1)
        x0, parts0 = solve_part(right[:HALF] - dot_tall(off_s[panel], parts1), panel, 0)
        L[slot, :HALF] = parts0[0]
        add_product(k, panel, 0, parts0[0])
        after(0)
        lanes = pl.ds(pl.multiple_of(k * W, 128), W)
        for i in range(16):

            @pl.when(c == i)
            def _():
                out_ref[:, lanes] = (x0, x1)[i // 8][32 * (i % 8) : 32 * (i % 8) + 32]

        return parts0, parts1

    far = lax.rem(y + 2, 4)

    def reduce_copies(panel, first, last):
        part = lambda buffer, i, rows: buffer.at[panel, i, rows]
        top, low, to_p, to_m = pl.ds(0, 32), pl.ds(32, 32), to[2][0], to[2][1]
        moves = [(acc.at[panel, q, 1 - core], XB.at[panel, q], other) for q in range(4)] + [
            (part(PB, far, top), HB.at[panel, 0], to_p),
            (part(PB, far, low), HB.at[panel, 1], to_m),
            (part(PB, y_p, low), part(FB, 0, low), to_p),
            (part(PB, y_m, top), part(FB, 1, top), to_m),
            (part(PB, y_p, top), part(FB, 0, top), to_p),
            (part(PB, y_m, low), part(FB, 1, low), to_m),
        ]
        return [
            pltpu.make_async_remote_copy(
                src, dst, rs_send.at[panel, i], rs_recv.at[panel, i], device_id=device, device_id_type=MESH
            )
            for i, (src, dst, device) in list(enumerate(moves))[first:last]
        ]

    def start(panel, first, last):
        for copy in reduce_copies(panel, first, last):
            copy.start()

    def arrive(panel, first, last):
        for copy in reduce_copies(panel, first, last):
            copy.wait_recv()

    def reduce_step(panel, s, out_ref):
        if s == 0:
            start(panel, 0, 4)
        elif s == 1:
            for i, q in enumerate((far, y_p, y_m, y)):
                pltpu.make_async_remote_copy(
                    acc.at[panel, q, 1 - core], XB.at[panel, q], rs_send.at[panel, q], rs_recv.at[panel, q],
                    device_id=other, device_id_type=MESH,
                ).wait_recv()
                PB[panel, q] = acc[panel, q, core] + XB[panel, q]
                if i == 0:
                    start(panel, 4, 6)
                elif i < 3:
                    start(panel, 5 + i, 6 + i)
        elif s == 2:
            arrive(panel, 4, 6)
            PB[panel, y_p, :32] += HB[panel, 0]
            PB[panel, y_m, 32:] += HB[panel, 1]
            start(panel, 8, 10)
        else:
            arrive(panel, 6, 10)
            out_ref[...] = CR[panel] - ((PB[panel, y] + FB[panel, 0]) + FB[panel, 1])

    def trail(k, panel):
        rows = pl.ds(pl.multiple_of(k * W, W), W)
        right = R[NB * panel : NB * panel + NB]
        update = lax.dot_general(L[lax.rem(k, 3)], right, (((0,), (0,)), ((), ())), preferred_element_type=F32)
        CT[rows] -= update

    @pl.loop(0, K)
    def _(k):
        communicate(k, (3, 2, 1, 0, 4))
        parts = chunk(k, 0, G[k].reshape(NB, W), ss_ref)
        trail(k, 0)
        T[k] = dot_tall(e_s[...], tuple(jnp.concatenate(p, axis=0) for p in zip(*parts)))

    @pl.loop(0, K - 1)
    def _(k):
        communicate(K + k, (3, 2, 1, 0))
        for s in range(4):

            @pl.when(k == s)
            def _():
                reduce_step(0, s, nrs_ref)

        @pl.when((k >= 1) & (k <= K - 3))
        def _():
            trail(k - 1, 1)

        communicate(K + k, (4,))
        chunk(k, 1, G[K + k].reshape(NB, W) - T[k], sf_ref)

    stage(N - 1, 4)
    chunk(K - 1, 1, G[N - 1].reshape(NB, W) - T[K - 1], sf_ref, lambda q: start(1, 2 * q, 2 * q + 2))
    trail(K - 3, 1)
    reduce_step(1, 1, nrf_ref)
    trail(K - 2, 1)
    reduce_step(1, 2, nrf_ref)
    trail(K - 1, 1)

    @pl.loop(0, N)
    def _(g):
        for s in range(4):
            for t in range(2):
                for d in range(2):
                    hop(g, t, s, d, False).wait_send()

    reduce_step(1, 3, nrf_ref)
    for panel in range(2):
        for copy in reduce_copies(panel, 0, 10):
            copy.wait_send()


def on_device(
    trail_rows, rows_first, rows_second, diag_first, diag_second, sub_block,
    cot_first, cot_second, cot_trail, cot_rows_first, cot_rows_second,
):
    rows, cols = trail_rows.shape
    K = rows // W
    shape = jax.ShapeDtypeStruct
    hbm = pl.BlockSpec(memory_space=pl.ANY)
    vmem = pl.BlockSpec(memory_space=pltpu.VMEM)
    dma = pltpu.SemaphoreType.DMA
    results = pl.pallas_call(
        kernel,
        out_shape=(
            pltpu.VMEM((rows, cols), F32),
            pltpu.VMEM((2, 64, cols), F32),
            pltpu.VMEM((2, 32, rows), F32),
        ),
        in_specs=[hbm] * 11,
        out_specs=(vmem,) * 3,
        scratch_shapes=[
            pltpu.VMEM((2 * K, 4, 4, 32, W), F32),
            pltpu.VMEM((K, NB, W), F32),
            pltpu.VMEM((3, NB, W), BF),
            pltpu.VMEM((rows, cols), BF),
            pltpu.VMEM((2 * NB, cols), BF),
            pltpu.VMEM((2, NB, NB), F32),
            pltpu.VMEM((NB, NB), F32),
            pltpu.VMEM((2, 4, 2, 64, cols), F32),
            pltpu.VMEM((2, 4, 64, cols), F32),
            pltpu.VMEM((2, 4, 64, cols), F32),
            pltpu.VMEM((2, 2, 32, cols), F32),
            pltpu.VMEM((2, 2, 64, cols), F32),
            pltpu.VMEM((2, 64, cols), F32),
            pltpu.VMEM((4, NB, HALF), BF),
            pltpu.VMEM((2, NB, HALF), BF),
            pltpu.VMEM((2 * NB, NB), BF),
            dma((2 * K,)),
            dma((9,)),
            dma((2 * K, 16)),
            dma((2 * K, 16)),
            dma((2, 10)),
            dma((2, 10)),
        ],
        compiler_params=pltpu.CompilerParams(
            collective_id=0, has_side_effects=True, vmem_limit_bytes=50 * 1024 * 1024
        ),
    )(
        cot_second.T, cot_first.T, trail_rows, rows_second, rows_first, diag_second, diag_first,
        sub_block, cot_trail, cot_rows_first, cot_rows_second,
    )
    new_trail, (new_first, new_second), (first_t, second_t) = results[0], results[1], results[2]
    return new_trail, new_first, new_second, first_t.T, second_t.T


def solution(mesh):
    both = P("row", "col")
    col = P(None, "col")
    return jax.shard_map(
        on_device,
        mesh=mesh,
        in_specs=(both, col, col, P(), P(), P(), both, both, both, both, both),
        out_specs=(both,) * 5,
        check_vma=False,
    )
```
